1024 devices in a mesh: dp: 64 (over y_lo, z), expert: 16 (over y_hi, x, core).
Axes of the slice: x: 4, y: 8 (y_hi: 2, y_lo: 4; y = y_hi * 4 + y_lo), z: 16, core: 2. Of those that a mesh axis runs over, the one named last changes fastest.
Arguments:
- tokens: bfloat16 [131072, 2048], P(('dp', 'expert')), may hold values from -24 to 24
- cotangent: bfloat16 [131072, 2048], P(('dp', 'expert')), may hold values from -12 to 12
- gate: float32 [131072, 1], P(('dp', 'expert')), may hold values from 0.1 to 1
- expert_ids: int32 [131072, 1], P(('dp', 'expert')), may hold values from 0 to 7; in each aligned block of 128 rows (0 to 127, 128 to 255, ...) at most 20 rows name the same one
- w_gate_up: bfloat16 [16, 2048, 768], P('expert'), may hold values from -0.125 to 0.125
- w_down: bfloat16 [16, 384, 2048], P('expert'), may hold values from -0.21875 to 0.21875
Outputs:
- input_grad: bfloat16 [131072, 2048], P(('dp', 'expert'))
- grad_down: float32 [16, 6144, 128], P('expert', 'dp')
The draws below stay inside these ranges and needn't reach their ends.
Inputs may be any that keep to these rules, and one draw needn't show every extreme that they name: `expert_ids`: each token has one route. Among the 128 tokens of one device (one aligned block of rows) at most 20 name the same expert, and in every draw some device has exactly 20 tokens naming one expert.
All inputs are finite; a program needn't handle non-finite values.
Results may differ from the reference program's by a relative error of at most 0.0065.
Values may be sent and summed in bfloat16 or wider, within the bound.
No kernel may reach another device: no remote copies, remote signals or barrier semaphores. Data moves between devices by JAX's collectives and lax.ppermute only.
A program may use at most 64 MiB of HBM per device.

```python
import math
import jax
import jax.numpy as jnp
import numpy as np
from jax import lax

D = 2048
HID_DEV = 384
TOPK = 1
TOK_DEV = 128
EXPERTS = 8
SLABS = 16
CAP = 20
TOKENS = 131072
N_DP = 64
N_EXPERT = 16


def raised(array, own_key, source, target, shards_of, factor):
    def block_of(dim):
        return (jnp.arange(array.shape[dim]) // (array.shape[dim] // shards_of)).reshape((-1,) + (1,) * (array.ndim - 1 - dim))

    one_side = jax.random.permutation(own_key, shards_of)[block_of(target)]
    other_side = (block_of(target) + shards_of // 2) % shards_of
    return jnp.where((block_of(source) == one_side) | (block_of(source) == other_side), factor * array, array)


def levels(key, dims, pieces, least, top_value):
    level, own = 1.0, jax.random.fold_in(key, 6)
    for position, blocks in pieces:
        draws = jnp.exp(jax.random.uniform(jax.random.fold_in(own, position), (blocks,), jnp.float32, least / len(pieces), top_value / len(pieces)))
        level = level * jnp.repeat(draws, dims[position] // blocks).reshape([-1 if axis == position else 1 for axis in range(len(dims))])
    return level


def shared_out(own_key, own, number, rows, amount, top, most, skew):
    ranking = jax.random.permutation(own_key, amount)
    heavy_load, common = load_shares(amount, rows * top, most, skew, True), load_shares(amount, rows * top, most, skew, False)
    places = jnp.arange(amount)

    def named(tallies, offset_by):
        used = int((tallies > 0).sum())
        fixed = max(1, used // 4)
        moved = fixed + (places - fixed + offset_by * (used - fixed)) % max(1, amount - fixed)
        return jnp.zeros((amount,), jnp.int32).at[ranking[jnp.where(places < fixed, places, moved)]].set(jnp.asarray(tallies, jnp.int32))

    tallies = jnp.where(number % 4 == 0, named(heavy_load, number // 4), named(common, number - number // 4 - 1))
    mixed = jax.random.permutation(jax.random.fold_in(own, 3), amount)
    donor, taker = mixed[0:amount // 2 * 2:2], mixed[1:amount // 2 * 2:2]
    slack = jnp.minimum(tallies[donor] - 1, most - tallies[taker]) // 2
    slack = jnp.where((donor == ranking[0]) | (taker == ranking[0]) | (tallies[taker] == 0), 0, jnp.maximum(slack, 0))
    moved = jax.random.randint(jax.random.fold_in(own, 4), (amount // 2,), 0, 1 << 20) % (slack + 1)
    tallies = tallies.at[donor].add(-moved).at[taker].add(moved)
    members = jnp.searchsorted(jnp.cumsum(tallies), jnp.arange(rows * top), side="right").astype(jnp.int32)
    listing = members.reshape(top, rows).T
    listing = listing[jax.random.permutation(jax.random.fold_in(own, 1), rows)]
    offset_by = jax.random.randint(jax.random.fold_in(own, 2), (rows, 1), 0, top)
    return jnp.take_along_axis(listing, (jnp.arange(top)[None, :] + offset_by) % top, axis=1)


def load_shares(amount, total, reach, skew, full):
    weights = [(1 << 20) // math.isqrt(standing ** skew) + 1 for standing in range(1, amount + 1)]
    largest = reach if full else min(reach, max(-(-total // amount), total * weights[0] // sum(weights)))
    least = 1 if total - largest >= amount - 1 else 0
    given, rest = [largest] + [least] * (amount - 1), total - largest - least * (amount - 1)
    while rest > 0:
        free = [i for i in range(1, amount) if given[i] < largest] or [i for i in range(1, amount) if given[i] < reach]
        pool, remaining = sum([weights[i] for i in free]), rest
        for i in free:
            extra = min(reach - given[i], max(1, remaining * weights[i] // pool), rest)
            given[i] = given[i] + extra
            rest = rest - extra
    return np.array(given)


def centred(rng, shape, spread, bound, pieces=(), kind=jnp.bfloat16):
    entries = jax.random.normal(rng, shape, jnp.float32) * spread
    if len(pieces) > 0:
        entries = levels(rng, shape, pieces, -0.22, 0.18) * entries
    return jnp.clip(entries, min=-bound, max=bound).astype(kind)


def noise_with(key, extent, width, limit, split, heavy, kind=jnp.bfloat16):
    drawn = width * jax.random.normal(key, extent, jnp.float32)
    if split:
        drawn = drawn * levels(key, extent, split, -0.22, 0.18)
    return jnp.clip(raised(drawn, jax.random.fold_in(key, 3), *heavy), -limit, limit).astype(kind)


def setup_inputs(seed: int = 0) -> dict:
    keys = jax.random.split(jax.random.key(seed), 7)
    tokens = noise_with(keys[0], (TOKENS, D), 1.0, 24.0, ((0, 1024),), (0, 1, 1024, 6.0))
    cotangent = noise_with(keys[1], (TOKENS, D), 0.5, 12.0, ((0, 1024),), (0, 1, 1024, 6.0))
    gate = jnp.clip(jnp.exp(math.log(1.0) - 2.3025851 * jax.random.uniform(keys[2], (TOKENS, TOPK), jnp.float32) ** levels(keys[2], (TOKENS, TOPK), ((0, 1024),), -0.2, 0.2)), 0.1, 1.0)
    expert_ids_keys = jax.random.split(jax.random.fold_in(keys[3], 1), TOKENS // TOK_DEV)
    expert_ids_turns = jax.random.permutation(jax.random.fold_in(keys[3], 3), TOKENS // TOK_DEV)
    expert_ids = jax.vmap(lambda own, number: shared_out(jax.random.fold_in(keys[3], 2), own, number, TOK_DEV, EXPERTS, TOPK, CAP, 2))(expert_ids_keys, expert_ids_turns).reshape((TOKENS, TOPK))
    w_gate_up = centred(keys[4], (SLABS, D, 2 * HID_DEV), D ** -0.5, 0.125, ((0, 16),))
    w_down = centred(keys[5], (SLABS, HID_DEV, D), (2 * HID_DEV) ** -0.5, 0.21875, ((0, 16),))
    return dict(tokens=tokens, cotangent=cotangent, gate=gate, expert_ids=expert_ids, w_gate_up=w_gate_up, w_down=w_down)


def slab_pass(token_rows, scaled_rows, gate_up_weight, down_weight):
    hidden_units = down_weight.shape[0]
    projected = jnp.dot(token_rows, gate_up_weight, preferred_element_type=jnp.float32)
    pre_gate = projected[:, :hidden_units]
    pre_up = projected[:, hidden_units:]
    squashed = jax.nn.sigmoid(pre_gate)
    swished = pre_gate * squashed
    hidden = (swished * pre_up).astype(jnp.bfloat16)
    hidden_grad = jnp.dot(scaled_rows, down_weight.T, preferred_element_type=jnp.float32)
    gate_part = hidden_grad * pre_up * squashed * (1.0 + pre_gate * (1.0 - squashed))
    pre_grad = jnp.concatenate([gate_part, hidden_grad * swished], axis=1).astype(jnp.bfloat16)
    partial_value = jnp.dot(pre_grad, gate_up_weight.T, preferred_element_type=jnp.float32).astype(jnp.bfloat16)
    down_term = jnp.dot(hidden.T, scaled_rows, preferred_element_type=jnp.float32)
    return partial_value, down_term


def reference(tokens, cotangent, gate, expert_ids, w_gate_up, w_down):
    scaled = (gate * cotangent.astype(jnp.float32)).astype(jnp.bfloat16)
    padding = jnp.zeros((1, D), jnp.bfloat16)
    token_rows = jnp.concatenate([tokens, padding], axis=0)
    scaled_rows = jnp.concatenate([scaled, padding], axis=0)
    routed = expert_ids[:, 0]
    most_rows = N_DP * N_EXPERT * CAP

    def scan_step(totals, expert_index):
        row_index = jnp.nonzero(routed == expert_index, size=most_rows, fill_value=TOKENS)[0]
        picked_rows = token_rows[row_index]
        picked_scaled = scaled_rows[row_index]
        first_slab = 2 * expert_index
        first_part, first_term = slab_pass(picked_rows, picked_scaled, w_gate_up[first_slab], w_down[first_slab])
        second_part, second_term = slab_pass(picked_rows, picked_scaled, w_gate_up[first_slab + 1], w_down[first_slab + 1])
        joined = (first_part.astype(jnp.float32) + second_part.astype(jnp.float32)).astype(jnp.bfloat16)
        totals = totals.at[row_index].set(joined, mode="drop")
        stacked = jnp.stack([first_term, second_term]) / N_DP
        return totals, stacked

    initial = jnp.zeros((TOKENS, D), jnp.bfloat16)
    input_grad, terms = lax.scan(scan_step, initial, jnp.arange(EXPERTS, dtype=jnp.int32))
    grad_down = terms.reshape(N_EXPERT, HID_DEV * D // 128, 128)
    return input_grad, grad_down
```

```python
import jax
import jax.numpy as jnp
from jax import lax
from jax.sharding import Mesh
from jax.sharding import PartitionSpec as P

Y_LO, Z, Y_HI, X, CORE = 4, 16, 2, 4, 2
DP = ("y_lo", "z")
CHIPS = ("y_hi", "x")
N_EXPERT = Y_HI * X
CAP = 20
OVER_ROWS = (((0,), (0,)), ((), ()))
OVER_COLUMNS = (((1,), (1,)), ((), ()))


def chips_exchange(block):
    return lax.all_to_all(block, CHIPS, split_axis=0, concat_axis=0, tiled=True)


def other_core(block):
    return lax.ppermute(block, "core", [(0, 1), (1, 0)])


def on_device(tokens, cotangent, gate, expert_ids, w_gate_up, w_down):
    tok_count, width = tokens.shape
    hidden_units = w_down.shape[1]
    rows = N_EXPERT * CAP

    routed = expert_ids[:, 0]
    onehot = (routed[:, None] == jnp.arange(N_EXPERT, dtype=jnp.int32)[None, :]).astype(jnp.int32)
    earlier = jnp.cumsum(onehot, axis=0) - onehot
    rank = jnp.sum(earlier * onehot, axis=1)

    scaled = (gate * cotangent.astype(jnp.float32)).astype(jnp.bfloat16)
    first = routed * (2 * CAP) + rank
    wanted = jnp.concatenate([first, first + CAP])
    placing = (jnp.arange(2 * rows, dtype=jnp.int32)[:, None] == wanted[None, :]).astype(
        jnp.bfloat16
    )
    placed = jnp.dot(
        placing, jnp.concatenate([tokens, scaled], axis=0), preferred_element_type=jnp.float32
    ).astype(jnp.bfloat16)
    mine = chips_exchange(placed.reshape(N_EXPERT, 2 * CAP, width))
    theirs = other_core(mine)
    both = jnp.concatenate([mine, theirs], axis=0)
    all_rows = both[:, :CAP].reshape(2 * rows, width)
    all_grads = both[:, CAP:].reshape(2 * rows, width)

    weight_in = w_gate_up[0]
    weight_out = w_down[0]
    projected = jnp.dot(all_rows, weight_in, preferred_element_type=jnp.float32)
    pre_gate = projected[:, :hidden_units]
    pre_up = projected[:, hidden_units:]
    squashed = jax.nn.sigmoid(pre_gate)
    swished = pre_gate * squashed
    hidden = (swished * pre_up).astype(jnp.bfloat16)
    term = lax.dot_general(hidden, all_grads, OVER_ROWS, preferred_element_type=jnp.float32)
    term = (term * (1.0 / (Y_LO * Z))).astype(jnp.bfloat16)

    by_y = lax.all_to_all(
        term.reshape(Y_LO, hidden_units // Y_LO, width), "y_lo", split_axis=0, concat_axis=0, tiled=True
    )
    y_sum = jnp.sum(by_y.astype(jnp.float32), axis=0).astype(jnp.bfloat16)
    y_sum = y_sum.reshape(Z, hidden_units * width // (128 * Y_LO * Z), 128)
    by_z = lax.all_to_all(y_sum, "z", split_axis=0, concat_axis=0, tiled=True)
    down_sum = jnp.sum(by_z.astype(jnp.float32), axis=0)

    hidden_grad = lax.dot_general(
        all_grads, weight_out, OVER_COLUMNS, preferred_element_type=jnp.float32
    )
    gate_part = hidden_grad * pre_up * squashed * (1.0 + pre_gate * (1.0 - squashed))
    pre_grad = jnp.concatenate([gate_part, hidden_grad * swished], axis=1).astype(jnp.bfloat16)
    partial = lax.dot_general(
        pre_grad, weight_in, OVER_COLUMNS, preferred_element_type=jnp.float32
    ).astype(jnp.bfloat16)
    received = other_core(partial[rows:])
    joined = (partial[:rows].astype(jnp.float32) + received.astype(jnp.float32)).astype(
        jnp.bfloat16
    )
    returned = chips_exchange(joined.reshape(N_EXPERT, CAP, width)).reshape(rows, width)
    taking = (
        jnp.arange(rows, dtype=jnp.int32)[:, None] == (routed * CAP + rank)[None, :]
    ).astype(jnp.bfloat16)
    input_grad = lax.dot_general(
        taking, returned, OVER_ROWS, preferred_element_type=jnp.float32
    ).astype(jnp.bfloat16)
    return (input_grad, down_sum[None])


def solution(mesh):
    fine = Mesh(
        mesh.devices.reshape(Y_LO, Z, Y_HI, X, CORE), ("y_lo", "z", "y_hi", "x", "core")
    )
    tok = P(("y_lo", "z", "y_hi", "x", "core"), None)
    slab = P(("y_hi", "x", "core"), None, None)
    return jax.shard_map(
        on_device,
        mesh=fine,
        in_specs=(tok, tok, tok, tok, slab, slab),
        out_specs=(tok, P(("y_hi", "x", "core"), DP, None)),
        check_vma=False,
    )
```

```python
import jax
import jax.numpy as jnp
from jax import lax
from jax.sharding import Mesh
from jax.sharding import PartitionSpec as P

AXES = dict(y_a=2, y_b=2, z_f=4, z_m=2, z_b=2, y_hi=2, x=4, core=2)
ALL = tuple(AXES)
DP = ("y_a", "y_b", "z_f", "z_m", "z_b")
NEAR, MID, FAR = ("y_b", "z_b"), ("y_a", "z_m"), "z_f"
N_DP = 64
X = 4
Y_LO = 4
N_EXPERT = 8
CAP = 20
OVER_ROWS = (((0,), (0,)), ((), ()))
OVER_COLUMNS = (((1,), (1,)), ((), ()))


GROUPS = [
    [(y * 2) * X + x for x in range(X)] + [((Y_LO - 1 - y) * 2 + 1) * X + x for x in range(X)]
    for y in range(Y_LO)
]


def chips_exchange(block):
    return lax.all_to_all(
        block,
        ("y_a", "y_b", "y_hi", "x"),
        split_axis=0,
        concat_axis=0,
        tiled=True,
        axis_index_groups=GROUPS,
    )


def other_core(block):
    return lax.ppermute(block, "core", [(0, 1), (1, 0)])


def shared(blocks, axes, routes):
    total = blocks[0].astype(jnp.float32)
    for block, route in zip(blocks[1:], routes):
        total = total + lax.ppermute(block, axes, route).astype(jnp.float32)
    return total


FLIPS = [[(i, i ^ k) for i in range(4)] for k in (1, 2, 3)]
TURNS = [[(i, (i + k) % 4) for i in range(4)] for k in (1, 2, 3)]


def shard_order(hidden_units):
    share = hidden_units // N_DP
    place = jnp.arange(hidden_units, dtype=jnp.int32)
    unit, place = place % share, place // share
    far, place = place % 4, place // 4
    mid, near = place % 4, place // 4
    y_b = lax.axis_index("y_b") ^ (near // 2)
    z_b = lax.axis_index("z_b") ^ (near % 2)
    y_a = lax.axis_index("y_a") ^ (mid // 2)
    z_m = lax.axis_index("z_m") ^ (mid % 2)
    z_f = (lax.axis_index("z_f") + far) % 4
    return ((((y_a * 2 + y_b) * 4 + z_f) * 2 + z_m) * 2 + z_b) * share + unit


def on_device(tokens, cotangent, gate, expert_ids, w_gate_up, w_down):
    tok_count, width = tokens.shape
    hidden_units = w_down.shape[1]
    rows = N_EXPERT * CAP

    routed = expert_ids[:, 0]
    onehot = (routed[:, None] == jnp.arange(N_EXPERT, dtype=jnp.int32)[None, :]).astype(jnp.int32)
    earlier = jnp.cumsum(onehot, axis=0) - onehot
    rank = jnp.sum(earlier * onehot, axis=1)

    scaled = (gate * cotangent.astype(jnp.float32)).astype(jnp.bfloat16)
    first = routed * (2 * CAP) + rank
    wanted = jnp.concatenate([first, first + CAP])
    placing = (jnp.arange(2 * rows, dtype=jnp.int32)[:, None] == wanted[None, :]).astype(
        jnp.bfloat16
    )
    placed = jnp.dot(
        placing, jnp.concatenate([tokens, scaled], axis=0), preferred_element_type=jnp.float32
    ).astype(jnp.bfloat16)
    mine = chips_exchange(placed.reshape(N_EXPERT, 2 * CAP, width))
    theirs = other_core(mine)
    both = jnp.concatenate([mine, theirs], axis=0)
    all_rows = both[:, :CAP].reshape(2 * rows, width)
    all_grads = both[:, CAP:].reshape(2 * rows, width)

    weight_in = w_gate_up[0]
    weight_out = w_down[0]
    projected = jnp.dot(all_rows, weight_in, preferred_element_type=jnp.float32)
    pre_gate = projected[:, :hidden_units]
    pre_up = projected[:, hidden_units:]
    squashed = jax.nn.sigmoid(pre_gate)
    swished = pre_gate * squashed
    hidden = (swished * pre_up).astype(jnp.bfloat16)
    reorder = (
        jnp.arange(hidden_units, dtype=jnp.int32)[:, None] == shard_order(hidden_units)[None, :]
    ).astype(jnp.bfloat16)
    hidden = jnp.dot(hidden, reorder, preferred_element_type=jnp.float32).astype(jnp.bfloat16)
    term = lax.dot_general(hidden, all_grads, OVER_ROWS, preferred_element_type=jnp.float32)
    term = term.astype(jnp.bfloat16)

    near = shared(jnp.split(term, 4), NEAR, FLIPS).astype(jnp.bfloat16)
    middle = shared(jnp.split(near, 4), MID, FLIPS).astype(jnp.bfloat16)
    down_sum = shared(jnp.split(middle, 4), FAR, TURNS) * (1.0 / N_DP)
    down_sum = down_sum.reshape(hidden_units * width // (128 * N_DP), 128)

    hidden_grad = lax.dot_general(
        all_grads, weight_out, OVER_COLUMNS, preferred_element_type=jnp.float32
    )
    gate_part = hidden_grad * pre_up * squashed * (1.0 + pre_gate * (1.0 - squashed))
    pre_grad = jnp.concatenate([gate_part, hidden_grad * swished], axis=1).astype(jnp.bfloat16)
    partial = lax.dot_general(
        pre_grad, weight_in, OVER_COLUMNS, preferred_element_type=jnp.float32
    ).astype(jnp.bfloat16)
    received = other_core(partial[rows:])
    joined = (partial[:rows].astype(jnp.float32) + received.astype(jnp.float32)).astype(
        jnp.bfloat16
    )
    returned = chips_exchange(joined.reshape(N_EXPERT, CAP, width)).reshape(rows, width)
    taking = (
        jnp.arange(rows, dtype=jnp.int32)[:, None] == (routed * CAP + rank)[None, :]
    ).astype(jnp.bfloat16)
    input_grad = lax.dot_general(
        taking, returned, OVER_ROWS, preferred_element_type=jnp.float32
    ).astype(jnp.bfloat16)
    return (input_grad, down_sum[None])


def solution(mesh):
    fine = Mesh(mesh.devices.reshape(tuple(AXES.values())), ALL)
    tok = P(ALL, None)
    slab = P(("y_hi", "x", "core"), None, None)
    return jax.shard_map(
        on_device,
        mesh=fine,
        in_specs=(tok, tok, tok, tok, slab, slab),
        out_specs=(tok, P(("y_hi", "x", "core"), DP, None)),
        check_vma=False,
    )
```

```python
import jax
import jax.numpy as jnp
from jax import lax
from jax.sharding import Mesh
from jax.sharding import PartitionSpec as P

AXES = dict(y_a=2, y_b=2, z_a=8, z_b=2, y_hi=2, x=4, core=2)
ALL = tuple(AXES)
DP = ("y_a", "y_b", "z_a", "z_b")
NEAR, FAR = ("y_b", "z_b"), ("y_a", "z_a")
N_DP = 64
X = 4
Y_LO = 4
N_EXPERT = 8
CAP = 20
OVER_ROWS = (((0,), (0,)), ((), ()))
OVER_COLUMNS = (((1,), (1,)), ((), ()))


GROUPS = [
    [(y * 2) * X + x for x in range(X)] + [((Y_LO - 1 - y) * 2 + 1) * X + x for x in range(X)]
    for y in range(Y_LO)
]


def chips_exchange(block):
    return lax.all_to_all(
        block,
        ("y_a", "y_b", "y_hi", "x"),
        split_axis=0,
        concat_axis=0,
        tiled=True,
        axis_index_groups=GROUPS,
    )


def other_core(block):
    return lax.ppermute(block, "core", [(0, 1), (1, 0)])


def shared(blocks, axes, routes):
    total = blocks[0].astype(jnp.float32)
    for block, route in zip(blocks[1:], routes):
        total = total + lax.ppermute(block, axes, route).astype(jnp.float32)
    return total


FLIPS = [[(i, i ^ k) for i in range(4)] for k in (1, 2, 3)]


def shard_order(hidden_units):
    share = hidden_units // N_DP
    place = jnp.arange(hidden_units, dtype=jnp.int32)
    unit, place = place % share, place // share
    far, near = place % 16, place // 16
    y_b = lax.axis_index("y_b") ^ (near // 2)
    z_b = lax.axis_index("z_b") ^ (near % 2)
    return ((((far // 8) * 2 + y_b) * 8 + far % 8) * 2 + z_b) * share + unit


def on_device(tokens, cotangent, gate, expert_ids, w_gate_up, w_down):
    tok_count, width = tokens.shape
    hidden_units = w_down.shape[1]
    rows = N_EXPERT * CAP

    routed = expert_ids[:, 0]
    onehot = (routed[:, None] == jnp.arange(N_EXPERT, dtype=jnp.int32)[None, :]).astype(jnp.int32)
    earlier = jnp.cumsum(onehot, axis=0) - onehot
    rank = jnp.sum(earlier * onehot, axis=1)

    scaled = (gate * cotangent.astype(jnp.float32)).astype(jnp.bfloat16)
    first = routed * (2 * CAP) + rank
    wanted = jnp.concatenate([first, first + CAP])
    placing = (jnp.arange(2 * rows, dtype=jnp.int32)[:, None] == wanted[None, :]).astype(
        jnp.bfloat16
    )
    placed = jnp.dot(
        placing, jnp.concatenate([tokens, scaled], axis=0), preferred_element_type=jnp.float32
    ).astype(jnp.bfloat16)
    mine = chips_exchange(placed.reshape(N_EXPERT, 2 * CAP, width))
    theirs = other_core(mine)
    both = jnp.concatenate([mine, theirs], axis=0)
    all_rows = both[:, :CAP].reshape(2 * rows, width)
    all_grads = both[:, CAP:].reshape(2 * rows, width)

    weight_in = w_gate_up[0]
    weight_out = w_down[0]
    projected = jnp.dot(all_rows, weight_in, preferred_element_type=jnp.float32)
    pre_gate = projected[:, :hidden_units]
    pre_up = projected[:, hidden_units:]
    squashed = jax.nn.sigmoid(pre_gate)
    swished = pre_gate * squashed
    hidden = (swished * pre_up).astype(jnp.bfloat16)
    reorder = (
        jnp.arange(hidden_units, dtype=jnp.int32)[:, None] == shard_order(hidden_units)[None, :]
    ).astype(jnp.bfloat16)
    hidden = jnp.dot(hidden, reorder, preferred_element_type=jnp.float32).astype(jnp.bfloat16)
    term = lax.dot_general(hidden, all_grads, OVER_ROWS, preferred_element_type=jnp.float32)
    term = term.astype(jnp.bfloat16)

    near = shared(jnp.split(term, 4), NEAR, FLIPS).astype(jnp.bfloat16)
    near = near.reshape(16, hidden_units * width // (128 * N_DP), 128)

    hidden_grad = lax.dot_general(
        all_grads, weight_out, OVER_COLUMNS, preferred_element_type=jnp.float32
    )
    gate_part = hidden_grad * pre_up * squashed * (1.0 + pre_gate * (1.0 - squashed))
    pre_grad = jnp.concatenate([gate_part, hidden_grad * swished], axis=1).astype(jnp.bfloat16)
    partial = lax.dot_general(
        pre_grad, weight_in, OVER_COLUMNS, preferred_element_type=jnp.float32
    ).astype(jnp.bfloat16)
    received = other_core(partial[rows:])
    joined = (partial[:rows].astype(jnp.float32) + received.astype(jnp.float32)).astype(
        jnp.bfloat16
    )
    returned = chips_exchange(joined.reshape(N_EXPERT, CAP, width)).reshape(rows, width)
    near, returned = lax.optimization_barrier((near, returned))
    far = lax.all_to_all(near, FAR, split_axis=0, concat_axis=0, tiled=True)
    down_sum = jnp.sum(far.astype(jnp.float32), axis=0) * (1.0 / N_DP)
    taking = (
        jnp.arange(rows, dtype=jnp.int32)[:, None] == (routed * CAP + rank)[None, :]
    ).astype(jnp.bfloat16)
    input_grad = lax.dot_general(
        taking, returned, OVER_ROWS, preferred_element_type=jnp.float32
    ).astype(jnp.bfloat16)
    return (input_grad, down_sum[None])


def solution(mesh):
    fine = Mesh(mesh.devices.reshape(tuple(AXES.values())), ALL)
    tok = P(ALL, None)
    slab = P(("y_hi", "x", "core"), None, None)
    return jax.shard_map(
        on_device,
        mesh=fine,
        in_specs=(tok, tok, tok, tok, slab, slab),
        out_specs=(tok, P(("y_hi", "x", "core"), DP, None)),
        check_vma=False,
    )
```

```python
import jax
import jax.numpy as jnp
from jax import lax
from jax.experimental import pallas as pl
from jax.experimental.pallas import tpu as pltpu
from jax.sharding import Mesh
from jax.sharding import PartitionSpec as P

AXES = dict(y_a=2, y_b=2, z_a=8, z_b=2, y_hi=2, x=4, core=2)
ALL = tuple(AXES)
DP = ("y_a", "y_b", "z_a", "z_b")
NEAR, FAR = ("y_b", "z_b"), ("y_a", "z_a")
N_DP = 64
X = 4
Y_LO = 4
N_EXPERT = 8
CAP = 20
MAIN = 16
TAIL = CAP - MAIN
CHUNK = 2 * CAP
ROWS = N_EXPERT * CAP
MAINS = N_EXPERT * MAIN
F32, BF16 = jnp.float32, jnp.bfloat16
OVER_ROWS = (((0,), (0,)), ((), ()))
OVER_COLUMNS = (((1,), (1,)), ((), ()))

GROUPS = [
    [(y * 2) * X + x for x in range(X)] + [((Y_LO - 1 - y) * 2 + 1) * X + x for x in range(X)]
    for y in range(Y_LO)
]
FLIPS = [[(i, i ^ k) for i in range(4)] for k in (1, 2, 3)]


def call(kernel, outs, *args, scratch=(), flops=0, far=(), limit=32 * 2**20):
    sizes = [a.size * a.dtype.itemsize for a in args]
    sizes += [o.size * o.dtype.itemsize for o in outs]
    return pl.pallas_call(
        kernel,
        out_shape=outs,
        in_specs=[
            pl.BlockSpec(memory_space=pltpu.HBM if i in far else pltpu.VMEM)
            for i in range(len(args))
        ],
        out_specs=[pl.BlockSpec(memory_space=pltpu.VMEM)] * len(outs),
        scratch_shapes=scratch,
        cost_estimate=pl.CostEstimate(flops=flops, bytes_accessed=sum(sizes), transcendentals=0),
        compiler_params=pltpu.CompilerParams(vmem_limit_bytes=limit),
        interpret=INTERPRET,
    )(*args)


INTERPRET = False


def out(shape, dtype=BF16):
    return jax.ShapeDtypeStruct(shape, dtype)


def fetch(sources, targets, semaphores):
    copies = [
        pltpu.make_async_copy(source, target, semaphores.at[i])
        for i, (source, target) in enumerate(zip(sources, targets))
    ]
    for copy in copies:
        copy.start()
    return copies


def token_slots(ids):
    tok_count = ids.shape[1]
    onehot = lax.broadcasted_iota(jnp.int32, (N_EXPERT, tok_count), 0) == ids
    onehot = jnp.where(onehot, 1.0, 0.0).astype(F32)
    before = lax.broadcasted_iota(jnp.int32, (tok_count, tok_count), 0) < lax.broadcasted_iota(
        jnp.int32, (tok_count, tok_count), 1
    )
    before = jnp.where(before, 1.0, 0.0).astype(F32)
    earlier = jnp.dot(onehot.astype(BF16), before.astype(BF16), preferred_element_type=F32)
    rank = jnp.sum(earlier * onehot, axis=0, keepdims=True).astype(jnp.int32)
    first = ids * CHUNK + rank + jnp.where(rank < MAIN, 0, MAIN)
    second = first + jnp.where(rank < MAIN, MAIN, TAIL)
    return first, second


def one_hot(slots):
    rows = lax.broadcasted_iota(jnp.int32, (N_EXPERT * CHUNK, slots.shape[1]), 0)
    return jnp.where(rows == slots, 1.0, 0.0).astype(BF16)


def place_kernel(*refs):
    sources, placed, targets, semaphores = refs[:4], refs[4], refs[5:9], refs[9]
    ids, gate, cotangent, tokens = targets
    copies = fetch(sources, targets, semaphores)
    tok_count = tokens.shape[0]
    copies[0].wait()
    first, second = token_slots(ids[...])
    copies[1].wait()
    column = jnp.transpose(jnp.broadcast_to(gate[...], (tok_count, tok_count)))[:, :1]
    copies[2].wait()
    scaled = (column * cotangent[...].astype(F32)).astype(BF16)
    value = jnp.dot(one_hot(second), scaled, preferred_element_type=F32)
    copies[3].wait()
    value = value + jnp.dot(one_hot(first), tokens[...], preferred_element_type=F32)
    placed[...] = value.astype(BF16)


def unplace_kernel(returned, ids, input_grad):
    half = returned.shape[1]
    for slots, low in zip(token_slots(ids[...]), (0, half)):
        value = lax.dot_general(
            one_hot(slots), returned[...], OVER_ROWS, preferred_element_type=F32
        )
        input_grad[:, low : low + half] = value.astype(BF16)


def upper_half(block):
    return lax.broadcasted_iota(jnp.int32, block.shape, 0) < TAIL


def slab_kernel(*refs):
    mine, theirs = refs[:2]
    part_mine, part_theirs, hidden, grads, rows = refs[4:9]
    weight_in, weight_out = refs[9:11]
    copies = fetch(refs[2:4], (weight_in, weight_out), refs[11])
    hidden_units = weight_out.shape[0]
    for half, source in enumerate((mine, theirs)):
        base = half * ROWS
        for i in range(N_EXPERT):
            at = CHUNK * i
            to = base + MAIN * i
            rows[to : to + MAIN] = source[at : at + MAIN]
            grads[to : to + MAIN] = source[at + MAIN : at + 2 * MAIN]
        row_tails, grad_tails = [], []
        for i in range(0, N_EXPERT, 2):
            at = CHUNK * i + 2 * MAIN
            even = source[at : at + 2 * TAIL].astype(F32)
            odd = source[at + CHUNK : at + CHUNK + 2 * TAIL].astype(F32)
            row_tails.append(jnp.where(upper_half(even), even, pltpu.roll(odd, TAIL, 0)))
            grad_tails.append(jnp.where(upper_half(even), pltpu.roll(even, TAIL, 0), odd))
        rows[base + MAINS : base + ROWS] = jnp.concatenate(row_tails, axis=0).astype(BF16)
        grads[base + MAINS : base + ROWS] = jnp.concatenate(grad_tails, axis=0).astype(BF16)
    copies[0].wait()
    projected = jnp.dot(rows[...], weight_in[...], preferred_element_type=F32)
    pre_gate = projected[:, :hidden_units]
    pre_up = projected[:, hidden_units:]
    squashed = jax.nn.sigmoid(pre_gate)
    swished = pre_gate * squashed
    hidden[...] = (swished * pre_up).astype(BF16)
    copies[1].wait()
    hidden_grad = lax.dot_general(
        grads[...], weight_out[...], OVER_COLUMNS, preferred_element_type=F32
    )
    gate_part = hidden_grad * pre_up * squashed * (1.0 + pre_gate * (1.0 - squashed))
    pre_grad = jnp.concatenate([gate_part, hidden_grad * swished], axis=1).astype(BF16)
    value = lax.dot_general(pre_grad, weight_in[...], OVER_COLUMNS, preferred_element_type=F32)
    part_mine[...] = value[:ROWS].astype(BF16)
    part_theirs[...] = value[ROWS:].astype(BF16)


def term_kernel(hidden, grads, reorder, *terms):
    turned = lax.dot_general(
        reorder[...], hidden[...], OVER_COLUMNS, preferred_element_type=F32
    ).astype(BF16)
    height = terms[0].shape[0]
    for k, term in enumerate(terms):
        term[...] = jnp.dot(
            turned[k * height : (k + 1) * height], grads[...], preferred_element_type=F32
        ).astype(BF16)


def join_kernel(mine, received, joined):
    half = joined.shape[1]

    def total(low, high, left, right):
        return mine[low:high, left:right].astype(F32) + received[low:high, left:right].astype(F32)

    for i in range(N_EXPERT):
        low, at = MAIN * i, CHUNK * i
        joined[at : at + MAIN] = total(low, low + MAIN, 0, half).astype(BF16)
        joined[at + MAIN : at + 2 * MAIN] = total(low, low + MAIN, half, 2 * half).astype(BF16)
    for i in range(0, N_EXPERT, 2):
        low, at = MAINS + TAIL * i, CHUNK * i + 2 * MAIN
        left = total(low, low + 2 * TAIL, 0, half)
        right = total(low, low + 2 * TAIL, half, 2 * half)
        even = jnp.where(upper_half(left), left, pltpu.roll(right, TAIL, 0))
        odd = jnp.where(upper_half(left), pltpu.roll(left, TAIL, 0), right)
        joined[at : at + 2 * TAIL] = even.astype(BF16)
        joined[at + CHUNK : at + CHUNK + 2 * TAIL] = odd.astype(BF16)


def chips_exchange(rows):
    block = rows.reshape(N_EXPERT, CHUNK, rows.shape[1])
    block = lax.all_to_all(
        block,
        ("y_a", "y_b", "y_hi", "x"),
        split_axis=0,
        concat_axis=0,
        tiled=True,
        axis_index_groups=GROUPS,
    )
    return block.reshape(rows.shape)


def other_core(block):
    return lax.ppermute(block, "core", [(0, 1), (1, 0)])


def shard_order(hidden_units):
    share = hidden_units // N_DP
    place = jnp.arange(hidden_units, dtype=jnp.int32)
    unit, place = place % share, place // share
    far, near = place % 16, place // 16
    y_b = lax.axis_index("y_b") ^ (near // 2)
    z_b = lax.axis_index("z_b") ^ (near % 2)
    return ((((far // 8) * 2 + y_b) * 8 + far % 8) * 2 + z_b) * share + unit


def on_device(tokens, cotangent, gate, expert_ids, w_gate_up, w_down):
    tok_count, width = tokens.shape
    hidden_units = w_down.shape[1]
    ids = expert_ids.reshape(1, tok_count)
    (placed,) = call(
        place_kernel,
        [out((N_EXPERT * CHUNK, width))],
        ids,
        gate.reshape(1, tok_count),
        cotangent,
        tokens,
        scratch=[
            pltpu.VMEM((1, tok_count), jnp.int32),
            pltpu.VMEM((1, tok_count), F32),
            pltpu.VMEM((tok_count, width), BF16),
            pltpu.VMEM((tok_count, width), BF16),
            pltpu.SemaphoreType.DMA((4,)),
        ],
        far=(0, 1, 2, 3),
        limit=67_000_000,
    )
    mine = chips_exchange(placed)
    theirs = other_core(mine)
    reorder = (
        shard_order(hidden_units)[:, None] == jnp.arange(hidden_units, dtype=jnp.int32)[None, :]
    ).astype(BF16)
    theirs, reorder = lax.optimization_barrier((theirs, reorder))

    matrix = 2 * 2 * ROWS * hidden_units * width
    part_mine, part_theirs, hidden, grads = call(
        slab_kernel,
        [
            out((ROWS, width)),
            out((ROWS, width)),
            out((2 * ROWS, hidden_units)),
            out((2 * ROWS, width)),
        ],
        mine,
        theirs,
        w_gate_up[0],
        w_down[0],
        scratch=[
            pltpu.VMEM((2 * ROWS, width), BF16),
            pltpu.VMEM((width, 2 * hidden_units), BF16),
            pltpu.VMEM((hidden_units, width), BF16),
            pltpu.SemaphoreType.DMA((2,)),
        ],
        flops=5 * matrix,
        far=(2, 3),
        limit=50_000_000,
    )
    received = other_core(part_theirs)
    terms = call(
        term_kernel, [out((hidden_units // 4, width))] * 4, hidden, grads, reorder, flops=matrix
    )
    received, terms = lax.optimization_barrier((received, terms))
    (joined,) = call(join_kernel, [out((N_EXPERT * CHUNK, width // 2))], part_mine, received)
    returned = chips_exchange(joined)

    near = terms[0].astype(F32)
    for term, route in zip(terms[1:], FLIPS):
        near = near + lax.ppermute(term, NEAR, route).astype(F32)
    near = near.astype(BF16).reshape(16, hidden_units * width // (128 * N_DP), 128)
    near, returned = lax.optimization_barrier((near, returned))
    far = lax.all_to_all(near, FAR, split_axis=0, concat_axis=0, tiled=True)
    down_sum = jnp.sum(far.astype(F32) * (1.0 / N_DP), axis=0)
    (input_grad,) = call(unplace_kernel, [out((tok_count, width))], returned, ids)
    return (input_grad, down_sum[None])


def solution(mesh):
    fine = Mesh(mesh.devices.reshape(tuple(AXES.values())), ALL)
    tok = P(ALL, None)
    slab = P(("y_hi", "x", "core"), None, None)
    return jax.shard_map(
        on_device,
        mesh=fine,
        in_specs=(tok, tok, tok, tok, slab, slab),
        out_specs=(tok, P(("y_hi", "x", "core"), DP, None)),
        check_vma=False,
    )
```

```python
import jax
import jax.numpy as jnp
from jax import lax
from jax.experimental import pallas as pl
from jax.experimental.pallas import tpu as pltpu
from jax.sharding import Mesh
from jax.sharding import PartitionSpec as P

AXES = dict(y_a=2, y_b=2, z_a=8, z_b=2, y_hi=2, x=4, core=2)
ALL = tuple(AXES)
DP = ("y_a", "y_b", "z_a", "z_b")
FAR = ("y_a", "z_a")
N_DP = 64
X = 4
Y_LO = 4
N_EXPERT = 8
CAP = 20
MAIN = 16
TAIL = CAP - MAIN
CHUNK = 2 * CAP
ROWS = N_EXPERT * CAP
MAINS = N_EXPERT * MAIN
F32, BF16 = jnp.float32, jnp.bfloat16
OVER_ROWS = (((0,), (0,)), ((), ()))
OVER_COLUMNS = (((1,), (1,)), ((), ()))

GROUPS = [
    [(y * 2) * X + x for x in range(X)] + [((Y_LO - 1 - y) * 2 + 1) * X + x for x in range(X)]
    for y in range(Y_LO)
]
ABOVE = [(z, z ^ 1) for z in range(16)]
BELOW = [(z, (z + 1) % 16 if z % 2 else (z - 1) % 16) for z in range(16)]


def call(kernel, outs, *args, scratch=(), flops=0, far=(), limit=32 * 2**20):
    sizes = [a.size * a.dtype.itemsize for a in args]
    sizes += [o.size * o.dtype.itemsize for o in outs]
    return pl.pallas_call(
        kernel,
        out_shape=outs,
        in_specs=[
            pl.BlockSpec(memory_space=pltpu.HBM if i in far else pltpu.VMEM)
            for i in range(len(args))
        ],
        out_specs=[pl.BlockSpec(memory_space=pltpu.VMEM)] * len(outs),
        scratch_shapes=scratch,
        cost_estimate=pl.CostEstimate(flops=flops, bytes_accessed=sum(sizes), transcendentals=0),
        compiler_params=pltpu.CompilerParams(vmem_limit_bytes=limit),
        interpret=INTERPRET,
    )(*args)


INTERPRET = False


def out(shape, dtype=BF16):
    return jax.ShapeDtypeStruct(shape, dtype)


def fetch(sources, targets, semaphores):
    copies = [
        pltpu.make_async_copy(source, target, semaphores.at[i])
        for i, (source, target) in enumerate(zip(sources, targets))
    ]
    for copy in copies:
        copy.start()
    return copies


def token_slots(ids):
    tok_count = ids.shape[1]
    onehot = lax.broadcasted_iota(jnp.int32, (N_EXPERT, tok_count), 0) == ids
    onehot = jnp.where(onehot, 1.0, 0.0).astype(F32)
    before = lax.broadcasted_iota(jnp.int32, (tok_count, tok_count), 0) < lax.broadcasted_iota(
        jnp.int32, (tok_count, tok_count), 1
    )
    before = jnp.where(before, 1.0, 0.0).astype(F32)
    earlier = jnp.dot(onehot.astype(BF16), before.astype(BF16), preferred_element_type=F32)
    rank = jnp.sum(earlier * onehot, axis=0, keepdims=True).astype(jnp.int32)
    first = ids * CHUNK + rank + jnp.where(rank < MAIN, 0, MAIN)
    second = first + jnp.where(rank < MAIN, MAIN, TAIL)
    return first, second


def one_hot(slots):
    rows = lax.broadcasted_iota(jnp.int32, (N_EXPERT * CHUNK, slots.shape[1]), 0)
    return jnp.where(rows == slots, 1.0, 0.0).astype(BF16)


def place_kernel(*refs):
    sources, placed, targets, semaphores = refs[:4], refs[4], refs[5:9], refs[9]
    ids, gate, cotangent, tokens = targets
    copies = fetch(sources, targets, semaphores)
    tok_count = tokens.shape[0]
    copies[0].wait()
    first, second = token_slots(ids[...])
    copies[1].wait()
    column = jnp.transpose(jnp.broadcast_to(gate[...], (tok_count, tok_count)))[:, :1]
    copies[2].wait()
    scaled = (column * cotangent[...].astype(F32)).astype(BF16)
    value = jnp.dot(one_hot(second), scaled, preferred_element_type=F32)
    copies[3].wait()
    value = value + jnp.dot(one_hot(first), tokens[...], preferred_element_type=F32)
    placed[...] = value.astype(BF16)


def unplace_kernel(returned, ids, input_grad):
    half = returned.shape[1]
    for slots, low in zip(token_slots(ids[...]), (0, half)):
        value = lax.dot_general(
            one_hot(slots), returned[...], OVER_ROWS, preferred_element_type=F32
        )
        input_grad[:, low : low + half] = value.astype(BF16)


def upper_half(block):
    return lax.broadcasted_iota(jnp.int32, block.shape, 0) < TAIL


def slab_kernel(*refs):
    mine, theirs = refs[:2]
    part_mine, part_theirs, hidden, grads, rows = refs[4:9]
    weight_in, weight_out = refs[9:11]
    copies = fetch(refs[2:4], (weight_in, weight_out), refs[11])
    hidden_units = weight_out.shape[0]
    for half, source in enumerate((mine, theirs)):
        base = half * ROWS
        for i in range(N_EXPERT):
            at = CHUNK * i
            to = base + MAIN * i
            rows[to : to + MAIN] = source[at : at + MAIN]
            grads[to : to + MAIN] = source[at + MAIN : at + 2 * MAIN]
        row_tails, grad_tails = [], []
        for i in range(0, N_EXPERT, 2):
            at = CHUNK * i + 2 * MAIN
            even = source[at : at + 2 * TAIL].astype(F32)
            odd = source[at + CHUNK : at + CHUNK + 2 * TAIL].astype(F32)
            row_tails.append(jnp.where(upper_half(even), even, pltpu.roll(odd, TAIL, 0)))
            grad_tails.append(jnp.where(upper_half(even), pltpu.roll(even, TAIL, 0), odd))
        rows[base + MAINS : base + ROWS] = jnp.concatenate(row_tails, axis=0).astype(BF16)
        grads[base + MAINS : base + ROWS] = jnp.concatenate(grad_tails, axis=0).astype(BF16)
    copies[0].wait()
    projected = jnp.dot(rows[...], weight_in[...], preferred_element_type=F32)
    pre_gate = projected[:, :hidden_units]
    pre_up = projected[:, hidden_units:]
    squashed = jax.nn.sigmoid(pre_gate)
    swished = pre_gate * squashed
    hidden[...] = (swished * pre_up).astype(BF16)
    copies[1].wait()
    hidden_grad = lax.dot_general(
        grads[...], weight_out[...], OVER_COLUMNS, preferred_element_type=F32
    )
    gate_part = hidden_grad * pre_up * squashed * (1.0 + pre_gate * (1.0 - squashed))
    pre_grad = jnp.concatenate([gate_part, hidden_grad * swished], axis=1).astype(BF16)
    value = lax.dot_general(pre_grad, weight_in[...], OVER_COLUMNS, preferred_element_type=F32)
    part_mine[...] = value[:ROWS].astype(BF16)
    part_theirs[...] = value[ROWS:].astype(BF16)


def term_kernel(hidden, grads, reorder, *terms):
    turned = lax.dot_general(
        reorder[...], hidden[...], OVER_COLUMNS, preferred_element_type=F32
    ).astype(BF16)
    height = terms[0].shape[0]
    for k, term in enumerate(terms):
        term[...] = jnp.dot(
            turned[k * height : (k + 1) * height], grads[...], preferred_element_type=F32
        ).astype(BF16)


def join_kernel(mine, received, joined):
    half = joined.shape[1]

    def total(low, high, left, right):
        return mine[low:high, left:right].astype(F32) + received[low:high, left:right].astype(F32)

    for i in range(N_EXPERT):
        low, at = MAIN * i, CHUNK * i
        joined[at : at + MAIN] = total(low, low + MAIN, 0, half).astype(BF16)
        joined[at + MAIN : at + 2 * MAIN] = total(low, low + MAIN, half, 2 * half).astype(BF16)
    for i in range(0, N_EXPERT, 2):
        low, at = MAINS + TAIL * i, CHUNK * i + 2 * MAIN
        left = total(low, low + 2 * TAIL, 0, half)
        right = total(low, low + 2 * TAIL, half, 2 * half)
        even = jnp.where(upper_half(left), left, pltpu.roll(right, TAIL, 0))
        odd = jnp.where(upper_half(left), pltpu.roll(left, TAIL, 0), right)
        joined[at : at + 2 * TAIL] = even.astype(BF16)
        joined[at + CHUNK : at + CHUNK + 2 * TAIL] = odd.astype(BF16)


def chips_exchange(rows):
    block = rows.reshape(N_EXPERT, CHUNK, rows.shape[1])
    block = lax.all_to_all(
        block,
        ("y_a", "y_b", "y_hi", "x"),
        split_axis=0,
        concat_axis=0,
        tiled=True,
        axis_index_groups=GROUPS,
    )
    return block.reshape(rows.shape)


def other_core(block):
    return lax.ppermute(block, "core", [(0, 1), (1, 0)])


def shard_order(hidden_units):
    share = hidden_units // N_DP
    place = jnp.arange(hidden_units, dtype=jnp.int32)
    unit, place = place % share, place // share
    far, near = place % 16, place // 16
    y_b = lax.axis_index("y_b") ^ (near % 2)
    z_b = lax.axis_index("z_b") ^ (near // 2)
    return ((((far // 8) * 2 + y_b) * 8 + far % 8) * 2 + z_b) * share + unit


def on_device(tokens, cotangent, gate, expert_ids, w_gate_up, w_down):
    tok_count, width = tokens.shape
    hidden_units = w_down.shape[1]
    ids = expert_ids.reshape(1, tok_count)
    (placed,) = call(
        place_kernel,
        [out((N_EXPERT * CHUNK, width))],
        ids,
        gate.reshape(1, tok_count),
        cotangent,
        tokens,
        scratch=[
            pltpu.VMEM((1, tok_count), jnp.int32),
            pltpu.VMEM((1, tok_count), F32),
            pltpu.VMEM((tok_count, width), BF16),
            pltpu.VMEM((tok_count, width), BF16),
            pltpu.SemaphoreType.DMA((4,)),
        ],
        far=(0, 1, 2, 3),
        limit=67_000_000,
    )
    mine = chips_exchange(placed)
    theirs = other_core(mine)
    reorder = (
        shard_order(hidden_units)[:, None] == jnp.arange(hidden_units, dtype=jnp.int32)[None, :]
    ).astype(BF16)
    theirs, reorder = lax.optimization_barrier((theirs, reorder))

    matrix = 2 * 2 * ROWS * hidden_units * width
    part_mine, part_theirs, hidden, grads = call(
        slab_kernel,
        [
            out((ROWS, width)),
            out((ROWS, width)),
            out((2 * ROWS, hidden_units)),
            out((2 * ROWS, width)),
        ],
        mine,
        theirs,
        w_gate_up[0],
        w_down[0],
        scratch=[
            pltpu.VMEM((2 * ROWS, width), BF16),
            pltpu.VMEM((width, 2 * hidden_units), BF16),
            pltpu.VMEM((hidden_units, width), BF16),
            pltpu.SemaphoreType.DMA((2,)),
        ],
        flops=5 * matrix,
        far=(2, 3),
        limit=50_000_000,
    )
    received = other_core(part_theirs)
    terms = call(
        term_kernel, [out((hidden_units // 4, width))] * 4, hidden, grads, reorder, flops=matrix
    )
    received, terms = lax.optimization_barrier((received, terms))
    (joined,) = call(join_kernel, [out((N_EXPERT * CHUNK, width // 2))], part_mine, received)
    returned = chips_exchange(joined)

    both = ("z_a", "z_b")
    below = lax.ppermute(terms[3], both, BELOW)
    above = lax.ppermute(terms[2], both, ABOVE)
    passed = (terms[1].astype(F32) + below.astype(F32)).astype(BF16)
    beside = lax.ppermute(passed, "y_b", [(0, 1), (1, 0)])
    near = terms[0].astype(F32) + above.astype(F32) + beside.astype(F32)
    near = near.astype(BF16).reshape(16, hidden_units * width // (128 * N_DP), 128)
    near, returned = lax.optimization_barrier((near, returned))
    far = lax.all_to_all(near, FAR, split_axis=0, concat_axis=0, tiled=True)
    down_sum = jnp.sum(far.astype(F32) * (1.0 / N_DP), axis=0)
    (input_grad,) = call(unplace_kernel, [out((tok_count, width))], returned, ids)
    return (input_grad, down_sum[None])


def solution(mesh):
    fine = Mesh(mesh.devices.reshape(tuple(AXES.values())), ALL)
    tok = P(ALL, None)
    slab = P(("y_hi", "x", "core"), None, None)
    return jax.shard_map(
        on_device,
        mesh=fine,
        in_specs=(tok, tok, tok, tok, slab, slab),
        out_specs=(tok, P(("y_hi", "x", "core"), DP, None)),
        check_vma=False,
    )
```

```python
import jax
import jax.numpy as jnp
from jax import lax
from jax.experimental import pallas as pl
from jax.experimental.pallas import tpu as pltpu
from jax.sharding import Mesh
from jax.sharding import PartitionSpec as P

AXES = dict(y_a=2, y_b=2, z_a=8, z_b=2, y_hi=2, x=4, core=2)
ALL = tuple(AXES)
DP = ("y_a", "y_b", "z_a", "z_b")
FAR = ("y_a", "z_a")
N_DP = 64
X = 4
Y_LO = 4
N_EXPERT = 8
CAP = 20
MAIN = 16
TAIL = CAP - MAIN
CHUNK = 2 * CAP
ROWS = N_EXPERT * CAP
MAINS = N_EXPERT * MAIN
F32, BF16 = jnp.float32, jnp.bfloat16
OVER_ROWS = (((0,), (0,)), ((), ()))
OVER_COLUMNS = (((1,), (1,)), ((), ()))

GROUP_AXES = ("y_a", "y_b", "y_hi", "x")
GROUPS = [
    [(y * 2) * X + x for x in range(X)] + [((Y_LO - 1 - y) * 2 + 1) * X + x for x in range(X)]
    for y in range(Y_LO)
]
ABOVE = [(z, z ^ 1) for z in range(16)]
BELOW = [(z, (z + 1) % 16 if z % 2 else (z - 1) % 16) for z in range(16)]


def call(kernel, outs, *args, scratch=(), flops=0, far=(), limit=32 * 2**20, scalars=0):
    sizes = [a.size * a.dtype.itemsize for a in args]
    sizes += [o.size * o.dtype.itemsize for o in outs]
    return pl.pallas_call(
        kernel,
        out_shape=outs,
        in_specs=[
            pl.BlockSpec(
                memory_space=pltpu.SMEM if i < scalars else pltpu.HBM if i in far else pltpu.VMEM
            )
            for i in range(len(args))
        ],
        out_specs=[pl.BlockSpec(memory_space=pltpu.VMEM)] * len(outs),
        scratch_shapes=scratch,
        cost_estimate=pl.CostEstimate(flops=flops, bytes_accessed=sum(sizes), transcendentals=0),
        compiler_params=pltpu.CompilerParams(vmem_limit_bytes=limit),
        interpret=INTERPRET,
    )(*args)


INTERPRET = False


def out(shape, dtype=BF16):
    return jax.ShapeDtypeStruct(shape, dtype)


def fetch(sources, targets, semaphores):
    copies = [
        pltpu.make_async_copy(source, target, semaphores.at[i])
        for i, (source, target) in enumerate(zip(sources, targets))
    ]
    for copy in copies:
        copy.start()
    return copies


def token_slots(ids):
    tok_count = ids.shape[1]
    onehot = lax.broadcasted_iota(jnp.int32, (N_EXPERT, tok_count), 0) == ids
    onehot = jnp.where(onehot, 1.0, 0.0).astype(F32)
    before = lax.broadcasted_iota(jnp.int32, (tok_count, tok_count), 0) < lax.broadcasted_iota(
        jnp.int32, (tok_count, tok_count), 1
    )
    before = jnp.where(before, 1.0, 0.0).astype(F32)
    earlier = jnp.dot(onehot.astype(BF16), before.astype(BF16), preferred_element_type=F32)
    rank = jnp.sum(earlier * onehot, axis=0, keepdims=True).astype(jnp.int32)
    first = ids * CHUNK + rank + jnp.where(rank < MAIN, 0, MAIN)
    second = first + jnp.where(rank < MAIN, MAIN, TAIL)
    return first, second


def one_hot(slots):
    rows = lax.broadcasted_iota(jnp.int32, (N_EXPERT * CHUNK, slots.shape[1]), 0)
    return jnp.where(rows == slots, 1.0, 0.0).astype(BF16)


def place_kernel(*refs):
    sources, placed, targets, semaphores = refs[:4], refs[4], refs[5:9], refs[9]
    ids, gate, cotangent, tokens = targets
    copies = fetch(sources, targets, semaphores)
    tok_count = tokens.shape[0]
    copies[0].wait()
    first, second = token_slots(ids[...])
    copies[1].wait()
    column = jnp.transpose(jnp.broadcast_to(gate[...], (tok_count, tok_count)))[:, :1]
    copies[2].wait()
    scaled = (column * cotangent[...].astype(F32)).astype(BF16)
    value = jnp.dot(one_hot(second), scaled, preferred_element_type=F32)
    copies[3].wait()
    value = value + jnp.dot(one_hot(first), tokens[...], preferred_element_type=F32)
    placed[...] = value.astype(BF16)


def unplace_kernel(ids, *refs):
    chunks, input_grad, returned = refs[:N_EXPERT], refs[N_EXPERT], refs[N_EXPERT + 1]
    half = returned.shape[1]
    for k, chunk in enumerate(chunks):
        returned[CHUNK * k : CHUNK * (k + 1)] = chunk[...]
    for slots, low in zip(token_slots(ids[...]), (0, half)):
        value = lax.dot_general(
            one_hot(slots), returned[...], OVER_ROWS, preferred_element_type=F32
        )
        input_grad[:, low : low + half] = value.astype(BF16)


def upper_half(block):
    return lax.broadcasted_iota(jnp.int32, block.shape, 0) < TAIL


def split_rows(source, rows, grads):
    for i in range(N_EXPERT):
        at, to = CHUNK * i, MAIN * i
        rows[to : to + MAIN] = source[at : at + MAIN]
        grads[to : to + MAIN] = source[at + MAIN : at + 2 * MAIN]
    row_tails, grad_tails = [], []
    for i in range(0, N_EXPERT, 2):
        at = CHUNK * i + 2 * MAIN
        even = source[at : at + 2 * TAIL].astype(F32)
        odd = source[at + CHUNK : at + CHUNK + 2 * TAIL].astype(F32)
        row_tails.append(jnp.where(upper_half(even), even, pltpu.roll(odd, TAIL, 0)))
        grad_tails.append(jnp.where(upper_half(even), pltpu.roll(even, TAIL, 0), odd))
    rows[MAINS:ROWS] = jnp.concatenate(row_tails, axis=0).astype(BF16)
    grads[MAINS:ROWS] = jnp.concatenate(grad_tails, axis=0).astype(BF16)


def project(rows, weight_in):
    projected = jnp.dot(rows[...], weight_in[...], preferred_element_type=F32)
    half = projected.shape[1] // 2
    pre_gate, pre_up = projected[:, :half], projected[:, half:]
    hidden = (pre_gate * jax.nn.sigmoid(pre_gate) * pre_up).astype(BF16)
    return projected, hidden


def own_kernel(source, weight_in, grads, projected, hidden, rows):
    split_rows(source, rows, grads)
    projected[...], hidden[...] = project(rows, weight_in)


def term_kernel(source, weight_in, own_hidden, own_grads, reorder, *refs):
    grads, projected, terms, rows, hidden = refs[0], refs[1], refs[2:6], refs[6], refs[7]
    both = refs[8]
    split_rows(source, rows, grads)
    hidden[:ROWS] = own_hidden[...]
    both[:ROWS] = own_grads[...]
    both[ROWS:] = grads[...]
    projected[...], hidden[ROWS:] = project(rows, weight_in)
    turned = lax.dot_general(
        reorder[...], hidden[...], OVER_COLUMNS, preferred_element_type=F32
    ).astype(BF16)
    height = terms[0].shape[0]
    for k, term in enumerate(terms):
        value = jnp.dot(
            turned[k * height : (k + 1) * height], both[...], preferred_element_type=F32
        )
        term[...] = value.astype(BF16)


def partial_kernel(*refs):
    weight_in, weight_out, parts, pre_grad = refs[4], refs[5], refs[6:8], refs[8]
    hidden_units = weight_out.shape[0]
    for k, (grads, projected) in enumerate((refs[0:2], refs[2:4])):
        pre_gate = projected[:, :hidden_units]
        pre_up = projected[:, hidden_units:]
        squashed = jax.nn.sigmoid(pre_gate)
        swished = pre_gate * squashed
        hidden_grad = lax.dot_general(
            grads[...], weight_out[...], OVER_COLUMNS, preferred_element_type=F32
        )
        gate_part = hidden_grad * pre_up * squashed * (1.0 + pre_gate * (1.0 - squashed))
        pre_grad[k * ROWS : (k + 1) * ROWS, :hidden_units] = gate_part.astype(BF16)
        pre_grad[k * ROWS : (k + 1) * ROWS, hidden_units:] = (hidden_grad * swished).astype(BF16)
    value = lax.dot_general(
        pre_grad[...], weight_in[...], OVER_COLUMNS, preferred_element_type=F32
    )
    parts[0][...] = value[:ROWS].astype(BF16)
    parts[1][...] = value[ROWS:].astype(BF16)


def join_kernel(place, mine, received, *chunks):
    half = chunks[0].shape[1]

    def total(low, high, left):
        rows, columns = pl.ds(low, high), slice(left, left + half)
        return mine[rows, columns].astype(F32) + received[rows, columns].astype(F32)

    for k, chunk in enumerate(chunks):
        i = place[0] ^ k
        low = pl.multiple_of(MAIN * i, MAIN)
        chunk[:MAIN] = total(low, MAIN, 0).astype(BF16)
        chunk[MAIN : 2 * MAIN] = total(low, MAIN, half).astype(BF16)
        low = pl.multiple_of(MAINS + 2 * TAIL * (i // 2), 2 * TAIL)
        left, right = total(low, 2 * TAIL, 0), total(low, 2 * TAIL, half)
        even = jnp.where(upper_half(left), left, pltpu.roll(right, TAIL, 0))
        odd = jnp.where(upper_half(left), pltpu.roll(left, TAIL, 0), right)
        chunk[2 * MAIN :] = jnp.where(i % 2 == 0, even, odd).astype(BF16)


def chips_exchange(rows):
    block = rows.reshape(N_EXPERT, CHUNK, rows.shape[1])
    block = lax.all_to_all(
        block,
        GROUP_AXES,
        split_axis=0,
        concat_axis=0,
        tiled=True,
        axis_index_groups=GROUPS,
    )
    return block.reshape(rows.shape)


def other_core(block):
    return lax.ppermute(block, "core", [(0, 1), (1, 0)])


def shard_order(hidden_units):
    share = hidden_units // N_DP
    place = jnp.arange(hidden_units, dtype=jnp.int32)
    unit, place = place % share, place // share
    far, near = place % 16, place // 16
    y_b = lax.axis_index("y_b") ^ (near % 2)
    z_b = lax.axis_index("z_b") ^ (near // 2)
    return ((((far // 8) * 2 + y_b) * 8 + far % 8) * 2 + z_b) * share + unit


def on_device(tokens, cotangent, gate, expert_ids, w_gate_up, w_down):
    tok_count, width = tokens.shape
    hidden_units = w_down.shape[1]
    ids = expert_ids.reshape(1, tok_count)
    (placed,) = call(
        place_kernel,
        [out((N_EXPERT * CHUNK, width))],
        ids,
        gate.reshape(1, tok_count),
        cotangent,
        tokens,
        scratch=[
            pltpu.VMEM((1, tok_count), jnp.int32),
            pltpu.VMEM((1, tok_count), F32),
            pltpu.VMEM((tok_count, width), BF16),
            pltpu.VMEM((tok_count, width), BF16),
            pltpu.SemaphoreType.DMA((4,)),
        ],
        far=(0, 1, 2, 3),
        limit=67_000_000,
    )
    mine = chips_exchange(placed)
    theirs = other_core(mine)
    reorder = (
        shard_order(hidden_units)[:, None] == jnp.arange(hidden_units, dtype=jnp.int32)[None, :]
    ).astype(BF16)
    theirs, reorder = lax.optimization_barrier((theirs, reorder))

    def vmem(rows, columns=width):
        return pltpu.VMEM((rows, columns), BF16)

    matrix = 2 * ROWS * hidden_units * width
    weight_in, weight_out = w_gate_up[0], w_down[0]
    kept = [out((ROWS, width)), out((ROWS, 2 * hidden_units), F32)]
    own_grads, own_projected, own_hidden = call(
        own_kernel,
        kept + [out((ROWS, hidden_units))],
        mine,
        weight_in,
        scratch=[vmem(ROWS)],
        flops=2 * matrix,
    )
    their_grads, their_projected, *terms = call(
        term_kernel,
        kept + [out((hidden_units // 4, width))] * 4,
        theirs,
        weight_in,
        own_hidden,
        own_grads,
        reorder,
        scratch=[vmem(ROWS), vmem(2 * ROWS, hidden_units), vmem(2 * ROWS)],
        flops=4 * matrix,
    )
    part_mine, part_theirs = call(
        partial_kernel,
        [out((ROWS, width))] * 2,
        own_grads,
        own_projected,
        their_grads,
        their_projected,
        weight_in,
        weight_out,
        scratch=[vmem(2 * ROWS, 2 * hidden_units)],
        flops=6 * matrix,
    )
    received = other_core(part_theirs)
    place = lax.axis_index("y_hi") * X + lax.axis_index("x")
    chunks = call(
        join_kernel,
        [out((CHUNK, width // 2))] * N_EXPERT,
        place.astype(jnp.int32)[None],
        part_mine,
        received,
        scalars=1,
    )
    returned = [chunks[0]]
    for k in range(1, N_EXPERT):
        route = [(g[i], g[i ^ k]) for g in GROUPS for i in range(N_EXPERT)]
        returned.append(lax.ppermute(chunks[k], GROUP_AXES, route))

    both = ("z_a", "z_b")
    below = lax.ppermute(terms[3], both, BELOW)
    above = lax.ppermute(terms[2], both, ABOVE)
    passed = (terms[1].astype(F32) + below.astype(F32)).astype(BF16)
    beside = lax.ppermute(passed, "y_b", [(0, 1), (1, 0)])
    near = terms[0].astype(F32) + above.astype(F32) + beside.astype(F32)
    near = near.astype(BF16).reshape(16, hidden_units * width // (128 * N_DP), 128)
    far = lax.all_to_all(near, FAR, split_axis=0, concat_axis=0, tiled=True)
    down_sum = jnp.sum(far.astype(F32) * (1.0 / N_DP), axis=0)
    (input_grad,) = call(
        unplace_kernel,
        [out((tok_count, width))],
        ids ^ place,
        *returned,
        scratch=[pltpu.VMEM((N_EXPERT * CHUNK, width // 2), BF16)],
    )
    return (input_grad, down_sum[None])


def solution(mesh):
    fine = Mesh(mesh.devices.reshape(tuple(AXES.values())), ALL)
    tok = P(ALL, None)
    slab = P(("y_hi", "x", "core"), None, None)
    return jax.shard_map(
        on_device,
        mesh=fine,
        in_specs=(tok, tok, tok, tok, slab, slab),
        out_specs=(tok, P(("y_hi", "x", "core"), DP, None)),
        check_vma=False,
    )
```

```python
import jax
import jax.numpy as jnp
from jax import lax
from jax.experimental import pallas as pl
from jax.experimental.pallas import tpu as pltpu
from jax.sharding import Mesh
from jax.sharding import PartitionSpec as P

AXES = dict(y_a=2, y_b=2, z_a=8, z_b=2, y_hi=2, x=4, core=2)
ALL = tuple(AXES)
DP = ("y_a", "y_b", "z_a", "z_b")
FAR = ("y_a", "z_a")
N_DP = 64
X = 4
Y_LO = 4
N_EXPERT = 8
CAP = 20
MAIN = 16
TAIL = CAP - MAIN
CHUNK = 2 * CAP
ROWS = N_EXPERT * CAP
MAINS = N_EXPERT * MAIN
F32, BF16 = jnp.float32, jnp.bfloat16
OVER_ROWS = (((0,), (0,)), ((), ()))
OVER_COLUMNS = (((1,), (1,)), ((), ()))

GROUP_AXES = ("y_a", "y_b", "y_hi", "x")
GROUPS = [
    [(y * 2) * X + x for x in range(X)] + [((Y_LO - 1 - y) * 2 + 1) * X + x for x in range(X)]
    for y in range(Y_LO)
]
ABOVE = [(z, z ^ 1) for z in range(16)]
BELOW = [(z, (z + 1) % 16 if z % 2 else (z - 1) % 16) for z in range(16)]


def call(kernel, outs, *args, scratch=(), flops=0, far=(), limit=32 * 2**20):
    sizes = [a.size * a.dtype.itemsize for a in args]
    sizes += [o.size * o.dtype.itemsize for o in outs]
    return pl.pallas_call(
        kernel,
        out_shape=outs,
        in_specs=[
            pl.BlockSpec(memory_space=pltpu.HBM if i in far else pltpu.VMEM)
            for i in range(len(args))
        ],
        out_specs=[pl.BlockSpec(memory_space=pltpu.VMEM)] * len(outs),
        scratch_shapes=scratch,
        cost_estimate=pl.CostEstimate(flops=flops, bytes_accessed=sum(sizes), transcendentals=0),
        compiler_params=pltpu.CompilerParams(vmem_limit_bytes=limit),
        interpret=INTERPRET,
    )(*args)


INTERPRET = False


def out(shape, dtype=BF16):
    return jax.ShapeDtypeStruct(shape, dtype)


def fetch(sources, targets, semaphores):
    copies = [
        pltpu.make_async_copy(source, target, semaphores.at[i])
        for i, (source, target) in enumerate(zip(sources, targets))
    ]
    for copy in copies:
        copy.start()
    return copies


def token_slots(ids):
    tok_count = ids.shape[1]
    onehot = lax.broadcasted_iota(jnp.int32, (N_EXPERT, tok_count), 0) == ids
    onehot = jnp.where(onehot, 1.0, 0.0).astype(F32)
    before = lax.broadcasted_iota(jnp.int32, (tok_count, tok_count), 0) < lax.broadcasted_iota(
        jnp.int32, (tok_count, tok_count), 1
    )
    before = jnp.where(before, 1.0, 0.0).astype(F32)
    earlier = jnp.dot(onehot.astype(BF16), before.astype(BF16), preferred_element_type=F32)
    rank = jnp.sum(earlier * onehot, axis=0, keepdims=True).astype(jnp.int32)
    first = ids * CHUNK + rank + jnp.where(rank < MAIN, 0, MAIN)
    second = first + jnp.where(rank < MAIN, MAIN, TAIL)
    return first, second


def one_hot(slots):
    rows = lax.broadcasted_iota(jnp.int32, (N_EXPERT * CHUNK, slots.shape[1]), 0)
    return jnp.where(rows == slots, 1.0, 0.0).astype(BF16)


def place_kernel(*refs):
    sources, placed, targets, semaphores = refs[:4], refs[4], refs[5:9], refs[9]
    ids, gate, cotangent, tokens = targets
    copies = fetch(sources, targets, semaphores)
    tok_count = tokens.shape[0]
    copies[0].wait()
    first, second = token_slots(ids[...])
    copies[1].wait()
    column = jnp.transpose(jnp.broadcast_to(gate[...], (tok_count, tok_count)))[:, :1]
    copies[2].wait()
    scaled = (column * cotangent[...].astype(F32)).astype(BF16)
    value = jnp.dot(one_hot(second), scaled, preferred_element_type=F32)
    copies[3].wait()
    value = value + jnp.dot(one_hot(first), tokens[...], preferred_element_type=F32)
    placed[...] = value.astype(BF16)


def unplace_kernel(returned, ids, input_grad):
    half = returned.shape[1]
    for slots, low in zip(token_slots(ids[...]), (0, half)):
        value = lax.dot_general(
            one_hot(slots), returned[...], OVER_ROWS, preferred_element_type=F32
        )
        input_grad[:, low : low + half] = value.astype(BF16)


def upper_half(block):
    return lax.broadcasted_iota(jnp.int32, block.shape, 0) < TAIL


def split_rows(source, rows, grads):
    for i in range(N_EXPERT):
        at, to = CHUNK * i, MAIN * i
        rows[to : to + MAIN] = source[at : at + MAIN]
        grads[to : to + MAIN] = source[at + MAIN : at + 2 * MAIN]
    row_tails, grad_tails = [], []
    for i in range(0, N_EXPERT, 2):
        at = CHUNK * i + 2 * MAIN
        even = source[at : at + 2 * TAIL].astype(F32)
        odd = source[at + CHUNK : at + CHUNK + 2 * TAIL].astype(F32)
        row_tails.append(jnp.where(upper_half(even), even, pltpu.roll(odd, TAIL, 0)))
        grad_tails.append(jnp.where(upper_half(even), pltpu.roll(even, TAIL, 0), odd))
    rows[MAINS:ROWS] = jnp.concatenate(row_tails, axis=0).astype(BF16)
    grads[MAINS:ROWS] = jnp.concatenate(grad_tails, axis=0).astype(BF16)


def project(rows, weight_in):
    projected = jnp.dot(rows[...], weight_in[...], preferred_element_type=F32)
    half = projected.shape[1] // 2
    pre_gate, pre_up = projected[:, :half], projected[:, half:]
    hidden = (pre_gate * jax.nn.sigmoid(pre_gate) * pre_up).astype(BF16)
    return projected, hidden


def own_kernel(source, weights, grads, projected, hidden, weight_in, rows, semaphores):
    copies = fetch((weights,), (weight_in,), semaphores)
    split_rows(source, rows, grads)
    copies[0].wait()
    projected[...], hidden[...] = project(rows, weight_in)


def term_kernel(source, weight_in, own_hidden, own_grads, reorder, *refs):
    grads, projected, terms, rows, hidden = refs[0], refs[1], refs[2:6], refs[6], refs[7]
    both = refs[8]
    split_rows(source, rows, grads)
    hidden[:ROWS] = own_hidden[...]
    both[:ROWS] = own_grads[...]
    both[ROWS:] = grads[...]
    projected[...], hidden[ROWS:] = project(rows, weight_in)
    turned = lax.dot_general(
        reorder[...], hidden[...], OVER_COLUMNS, preferred_element_type=F32
    ).astype(BF16)
    height = terms[0].shape[0]
    for k, term in enumerate(terms):
        value = jnp.dot(
            turned[k * height : (k + 1) * height], both[...], preferred_element_type=F32
        )
        term[...] = value.astype(BF16)


def partial_kernel(*refs):
    weight_in, weight_out, parts, pre_grad = refs[4], refs[5], refs[6:8], refs[8]
    hidden_units = weight_out.shape[0]
    for k, (grads, projected) in enumerate((refs[0:2], refs[2:4])):
        pre_gate = projected[:, :hidden_units]
        pre_up = projected[:, hidden_units:]
        squashed = jax.nn.sigmoid(pre_gate)
        swished = pre_gate * squashed
        hidden_grad = lax.dot_general(
            grads[...], weight_out[...], OVER_COLUMNS, preferred_element_type=F32
        )
        gate_part = hidden_grad * pre_up * squashed * (1.0 + pre_gate * (1.0 - squashed))
        pre_grad[k * ROWS : (k + 1) * ROWS, :hidden_units] = gate_part.astype(BF16)
        pre_grad[k * ROWS : (k + 1) * ROWS, hidden_units:] = (hidden_grad * swished).astype(BF16)
    value = lax.dot_general(
        pre_grad[...], weight_in[...], OVER_COLUMNS, preferred_element_type=F32
    )
    parts[0][...] = value[:ROWS].astype(BF16)
    parts[1][...] = value[ROWS:].astype(BF16)


def join_kernel(mine, received, joined):
    half = joined.shape[1]

    def total(low, high, left, right):
        return mine[low:high, left:right].astype(F32) + received[low:high, left:right].astype(F32)

    for i in range(N_EXPERT):
        low, at = MAIN * i, CHUNK * i
        joined[at : at + MAIN] = total(low, low + MAIN, 0, half).astype(BF16)
        joined[at + MAIN : at + 2 * MAIN] = total(low, low + MAIN, half, 2 * half).astype(BF16)
    for i in range(0, N_EXPERT, 2):
        low, at = MAINS + TAIL * i, CHUNK * i + 2 * MAIN
        left = total(low, low + 2 * TAIL, 0, half)
        right = total(low, low + 2 * TAIL, half, 2 * half)
        even = jnp.where(upper_half(left), left, pltpu.roll(right, TAIL, 0))
        odd = jnp.where(upper_half(left), pltpu.roll(left, TAIL, 0), right)
        joined[at : at + 2 * TAIL] = even.astype(BF16)
        joined[at + CHUNK : at + CHUNK + 2 * TAIL] = odd.astype(BF16)


def chips_exchange(rows):
    block = rows.reshape(N_EXPERT, CHUNK, rows.shape[1])
    block = lax.all_to_all(
        block,
        GROUP_AXES,
        split_axis=0,
        concat_axis=0,
        tiled=True,
        axis_index_groups=GROUPS,
    )
    return block.reshape(rows.shape)


def other_core(block):
    return lax.ppermute(block, "core", [(0, 1), (1, 0)])


def shard_order(hidden_units):
    share = hidden_units // N_DP
    place = jnp.arange(hidden_units, dtype=jnp.int32)
    unit, place = place % share, place // share
    far, near = place % 16, place // 16
    y_b = lax.axis_index("y_b") ^ (near % 2)
    z_b = lax.axis_index("z_b") ^ (near // 2)
    return ((((far // 8) * 2 + y_b) * 8 + far % 8) * 2 + z_b) * share + unit


def on_device(tokens, cotangent, gate, expert_ids, w_gate_up, w_down):
    tok_count, width = tokens.shape
    hidden_units = w_down.shape[1]
    ids = expert_ids.reshape(1, tok_count)
    (placed,) = call(
        place_kernel,
        [out((N_EXPERT * CHUNK, width))],
        ids,
        gate.reshape(1, tok_count),
        cotangent,
        tokens,
        scratch=[
            pltpu.VMEM((1, tok_count), jnp.int32),
            pltpu.VMEM((1, tok_count), F32),
            pltpu.VMEM((tok_count, width), BF16),
            pltpu.VMEM((tok_count, width), BF16),
            pltpu.SemaphoreType.DMA((4,)),
        ],
        far=(0, 1, 2, 3),
        limit=67_000_000,
    )
    mine = chips_exchange(placed)
    theirs = other_core(mine)
    reorder = (
        shard_order(hidden_units)[:, None] == jnp.arange(hidden_units, dtype=jnp.int32)[None, :]
    ).astype(BF16)
    theirs, reorder = lax.optimization_barrier((theirs, reorder))

    def vmem(rows, columns=width):
        return pltpu.VMEM((rows, columns), BF16)

    matrix = 2 * ROWS * hidden_units * width
    weight_out = w_down[0]
    kept = [out((ROWS, width)), out((ROWS, 2 * hidden_units), F32)]
    own_grads, own_projected, own_hidden, weight_in = call(
        own_kernel,
        kept + [out((ROWS, hidden_units)), out((width, 2 * hidden_units))],
        mine,
        w_gate_up[0],
        scratch=[vmem(ROWS), pltpu.SemaphoreType.DMA((1,))],
        flops=2 * matrix,
        far=(1,),
        limit=50_000_000,
    )
    their_grads, their_projected, *terms = call(
        term_kernel,
        kept + [out((hidden_units // 4, width))] * 4,
        theirs,
        weight_in,
        own_hidden,
        own_grads,
        reorder,
        scratch=[vmem(ROWS), vmem(2 * ROWS, hidden_units), vmem(2 * ROWS)],
        flops=4 * matrix,
    )
    part_mine, part_theirs = call(
        partial_kernel,
        [out((ROWS, width))] * 2,
        own_grads,
        own_projected,
        their_grads,
        their_projected,
        weight_in,
        weight_out,
        scratch=[vmem(2 * ROWS, 2 * hidden_units)],
        flops=6 * matrix,
    )
    received = other_core(part_theirs)
    (joined,) = call(join_kernel, [out((N_EXPERT * CHUNK, width // 2))], part_mine, received)
    returned = chips_exchange(joined)

    both = ("z_a", "z_b")
    below = lax.ppermute(terms[3], both, BELOW)
    above = lax.ppermute(terms[2], both, ABOVE)
    passed = (terms[1].astype(F32) + below.astype(F32)).astype(BF16)
    beside = lax.ppermute(passed, "y_b", [(0, 1), (1, 0)])
    near = terms[0].astype(F32) + above.astype(F32) + beside.astype(F32)
    near = near.astype(BF16).reshape(16, hidden_units * width // (128 * N_DP), 128)
    near, returned = lax.optimization_barrier((near, returned))
    far = lax.all_to_all(near, FAR, split_axis=0, concat_axis=0, tiled=True)
    down_sum = jnp.sum(far.astype(F32) * (1.0 / N_DP), axis=0)
    (input_grad,) = call(unplace_kernel, [out((tok_count, width))], returned, ids)
    return (input_grad, down_sum[None])


def solution(mesh):
    fine = Mesh(mesh.devices.reshape(tuple(AXES.values())), ALL)
    tok = P(ALL, None)
    slab = P(("y_hi", "x", "core"), None, None)
    return jax.shard_map(
        on_device,
        mesh=fine,
        in_specs=(tok, tok, tok, tok, slab, slab),
        out_specs=(tok, P(("y_hi", "x", "core"), DP, None)),
        check_vma=False,
    )
```

```python
import jax
import jax.numpy as jnp
from jax import lax
from jax.experimental import pallas as pl
from jax.experimental.pallas import tpu as pltpu
from jax.sharding import Mesh
from jax.sharding import PartitionSpec as P

AXES = dict(y_a=2, y_b=2, z_a=8, z_b=2, y_hi=2, x=4, core=2)
ALL = tuple(AXES)
DP = ("y_a", "y_b", "z_a", "z_b")
FAR = ("y_a", "z_a")
N_DP = 64
X = 4
Y_LO = 4
N_EXPERT = 8
CAP = 20
MAIN = 16
TAIL = CAP - MAIN
CHUNK = 2 * CAP
BLOCKS = 4
ROWS = N_EXPERT * CAP
MAINS = N_EXPERT * MAIN
F32, BF16 = jnp.float32, jnp.bfloat16
OVER_ROWS = (((0,), (0,)), ((), ()))
OVER_COLUMNS = (((1,), (1,)), ((), ()))

GROUP_AXES = ("y_a", "y_b", "y_hi", "x")
GROUPS = [
    [(y * 2) * X + x for x in range(X)] + [((Y_LO - 1 - y) * 2 + 1) * X + x for x in range(X)]
    for y in range(Y_LO)
]
ABOVE = [(z, z ^ 1) for z in range(16)]
BELOW = [(z, (z + 1) % 16 if z % 2 else (z - 1) % 16) for z in range(16)]


def call(kernel, outs, *args, scratch=(), flops=0, far=(), limit=32 * 2**20, kept=pltpu.VMEM):
    sizes = [a.size * a.dtype.itemsize for a in args]
    sizes += [o.size * o.dtype.itemsize for o in outs]
    return pl.pallas_call(
        kernel,
        out_shape=outs,
        in_specs=[
            pl.BlockSpec(memory_space=pltpu.HBM if i in far else pltpu.VMEM)
            for i in range(len(args))
        ],
        out_specs=[pl.BlockSpec(memory_space=kept)] * len(outs),
        scratch_shapes=scratch,
        cost_estimate=pl.CostEstimate(flops=flops, bytes_accessed=sum(sizes), transcendentals=0),
        compiler_params=pltpu.CompilerParams(vmem_limit_bytes=limit),
        interpret=INTERPRET,
    )(*args)


INTERPRET = False


def out(shape, dtype=BF16):
    return jax.ShapeDtypeStruct(shape, dtype)


def fetch(sources, targets, semaphores):
    copies = [
        pltpu.make_async_copy(source, target, semaphores.at[i])
        for i, (source, target) in enumerate(zip(sources, targets))
    ]
    for copy in copies:
        copy.start()
    return copies


def token_slots(ids):
    tok_count = ids.shape[1]
    onehot = lax.broadcasted_iota(jnp.int32, (N_EXPERT, tok_count), 0) == ids
    onehot = jnp.where(onehot, 1.0, 0.0).astype(F32)
    before = lax.broadcasted_iota(jnp.int32, (tok_count, tok_count), 0) < lax.broadcasted_iota(
        jnp.int32, (tok_count, tok_count), 1
    )
    before = jnp.where(before, 1.0, 0.0).astype(F32)
    earlier = jnp.dot(onehot.astype(BF16), before.astype(BF16), preferred_element_type=F32)
    rank = jnp.sum(earlier * onehot, axis=0, keepdims=True).astype(jnp.int32)
    first = ids * CHUNK + rank + jnp.where(rank < MAIN, 0, MAIN)
    second = first + jnp.where(rank < MAIN, MAIN, TAIL)
    return first, second


def one_hot(slots):
    rows = lax.broadcasted_iota(jnp.int32, (N_EXPERT * CHUNK, slots.shape[1]), 0)
    return jnp.where(rows == slots, 1.0, 0.0).astype(BF16)


def place_kernel(*refs):
    sources, placed = refs[:4], refs[4]
    ids, gate, cotangent, both, made, semaphores, done = refs[5:]
    tok_count = cotangent.shape[0]
    copies = fetch(sources, (ids, gate, cotangent, both.at[:tok_count]), semaphores)
    copies[0].wait()
    slots = jnp.concatenate(token_slots(ids[...]), axis=1)
    copies[1].wait()
    column = jnp.transpose(jnp.broadcast_to(gate[...], (tok_count, tok_count)))[:, :1]
    copies[2].wait()
    both[tok_count:] = (column * cotangent[...].astype(F32)).astype(BF16)
    copies[3].wait()
    onehot = one_hot(slots)
    height = made.shape[0] // BLOCKS
    writes = []
    for i in range(BLOCKS):
        block = slice(i * height, (i + 1) * height)
        value = jnp.dot(onehot[block], both[...], preferred_element_type=F32)
        made[block] = value.astype(BF16)
        writes.append(pltpu.make_async_copy(made.at[block], placed.at[block], done.at[i]))
        writes[-1].start()
    for write in writes:
        write.wait()


def unplace_kernel(returned, ids, input_grad):
    half = returned.shape[1]
    for slots, low in zip(token_slots(ids[...]), (0, half)):
        value = lax.dot_general(
            one_hot(slots), returned[...], OVER_ROWS, preferred_element_type=F32
        )
        input_grad[:, low : low + half] = value.astype(BF16)


def upper_half(block):
    return lax.broadcasted_iota(jnp.int32, block.shape, 0) < TAIL


def split_rows(source, rows, grads):
    for i in range(N_EXPERT):
        at, to = CHUNK * i, MAIN * i
        rows[to : to + MAIN] = source[at : at + MAIN]
        grads[to : to + MAIN] = source[at + MAIN : at + 2 * MAIN]
    row_tails, grad_tails = [], []
    for i in range(0, N_EXPERT, 2):
        at = CHUNK * i + 2 * MAIN
        even = source[at : at + 2 * TAIL].astype(F32)
        odd = source[at + CHUNK : at + CHUNK + 2 * TAIL].astype(F32)
        row_tails.append(jnp.where(upper_half(even), even, pltpu.roll(odd, TAIL, 0)))
        grad_tails.append(jnp.where(upper_half(even), pltpu.roll(even, TAIL, 0), odd))
    rows[MAINS:ROWS] = jnp.concatenate(row_tails, axis=0).astype(BF16)
    grads[MAINS:ROWS] = jnp.concatenate(grad_tails, axis=0).astype(BF16)


def project(rows, weight_in):
    projected = jnp.dot(rows[...], weight_in[...], preferred_element_type=F32)
    half = projected.shape[1] // 2
    pre_gate, pre_up = projected[:, :half], projected[:, half:]
    hidden = (pre_gate * jax.nn.sigmoid(pre_gate) * pre_up).astype(BF16)
    return projected, hidden


def own_kernel(source, weights, grads, projected, hidden, weight_in, rows, semaphores):
    copies = fetch((weights,), (weight_in,), semaphores)
    split_rows(source, rows, grads)
    copies[0].wait()
    projected[...], hidden[...] = project(rows, weight_in)


def term_kernel(source, weight_in, own_hidden, own_grads, reorder, *refs):
    grads, projected, terms, rows, hidden = refs[0], refs[1], refs[2:6], refs[6], refs[7]
    both = refs[8]
    split_rows(source, rows, grads)
    hidden[:ROWS] = own_hidden[...]
    both[:ROWS] = own_grads[...]
    both[ROWS:] = grads[...]
    projected[...], hidden[ROWS:] = project(rows, weight_in)
    turned = lax.dot_general(
        reorder[...], hidden[...], OVER_COLUMNS, preferred_element_type=F32
    ).astype(BF16)
    height = terms[0].shape[0]
    for k, term in enumerate(terms):
        value = jnp.dot(
            turned[k * height : (k + 1) * height], both[...], preferred_element_type=F32
        )
        term[...] = value.astype(BF16)


def partial_kernel(*refs):
    weight_in, weight_out, parts, pre_grad = refs[4], refs[5], refs[6:8], refs[8]
    hidden_units = weight_out.shape[0]
    for k, (grads, projected) in enumerate((refs[0:2], refs[2:4])):
        pre_gate = projected[:, :hidden_units]
        pre_up = projected[:, hidden_units:]
        squashed = jax.nn.sigmoid(pre_gate)
        swished = pre_gate * squashed
        hidden_grad = lax.dot_general(
            grads[...], weight_out[...], OVER_COLUMNS, preferred_element_type=F32
        )
        gate_part = hidden_grad * pre_up * squashed * (1.0 + pre_gate * (1.0 - squashed))
        pre_grad[k * ROWS : (k + 1) * ROWS, :hidden_units] = gate_part.astype(BF16)
        pre_grad[k * ROWS : (k + 1) * ROWS, hidden_units:] = (hidden_grad * swished).astype(BF16)
    value = lax.dot_general(
        pre_grad[...], weight_in[...], OVER_COLUMNS, preferred_element_type=F32
    )
    parts[0][...] = value[:ROWS].astype(BF16)
    parts[1][...] = value[ROWS:].astype(BF16)


def join_kernel(mine, received, joined):
    half = joined.shape[1]

    def total(low, high, left, right):
        return mine[low:high, left:right].astype(F32) + received[low:high, left:right].astype(F32)

    for i in range(N_EXPERT):
        low, at = MAIN * i, CHUNK * i
        joined[at : at + MAIN] = total(low, low + MAIN, 0, half).astype(BF16)
        joined[at + MAIN : at + 2 * MAIN] = total(low, low + MAIN, half, 2 * half).astype(BF16)
    for i in range(0, N_EXPERT, 2):
        low, at = MAINS + TAIL * i, CHUNK * i + 2 * MAIN
        left = total(low, low + 2 * TAIL, 0, half)
        right = total(low, low + 2 * TAIL, half, 2 * half)
        even = jnp.where(upper_half(left), left, pltpu.roll(right, TAIL, 0))
        odd = jnp.where(upper_half(left), pltpu.roll(left, TAIL, 0), right)
        joined[at : at + 2 * TAIL] = even.astype(BF16)
        joined[at + CHUNK : at + CHUNK + 2 * TAIL] = odd.astype(BF16)


def chips_exchange(rows):
    block = rows.reshape(N_EXPERT, CHUNK, rows.shape[1])
    block = lax.all_to_all(
        block,
        GROUP_AXES,
        split_axis=0,
        concat_axis=0,
        tiled=True,
        axis_index_groups=GROUPS,
    )
    return block.reshape(rows.shape)


def other_core(block):
    return lax.ppermute(block, "core", [(0, 1), (1, 0)])


def shard_order(hidden_units):
    share = hidden_units // N_DP
    place = jnp.arange(hidden_units, dtype=jnp.int32)
    unit, place = place % share, place // share
    far, near = place % 16, place // 16
    y_b = lax.axis_index("y_b") ^ (near % 2)
    z_b = lax.axis_index("z_b") ^ (near // 2)
    return ((((far // 8) * 2 + y_b) * 8 + far % 8) * 2 + z_b) * share + unit


def on_device(tokens, cotangent, gate, expert_ids, w_gate_up, w_down):
    tok_count, width = tokens.shape
    hidden_units = w_down.shape[1]
    ids = expert_ids.reshape(1, tok_count)
    (placed,) = call(
        place_kernel,
        [out((N_EXPERT * CHUNK, width))],
        ids,
        gate.reshape(1, tok_count),
        cotangent,
        tokens,
        scratch=[
            pltpu.VMEM((1, tok_count), jnp.int32),
            pltpu.VMEM((1, tok_count), F32),
            pltpu.VMEM((tok_count, width), BF16),
            pltpu.VMEM((2 * tok_count, width), BF16),
            pltpu.VMEM((N_EXPERT * CHUNK, width), BF16),
            pltpu.SemaphoreType.DMA((4,)),
            pltpu.SemaphoreType.DMA((BLOCKS,)),
        ],
        kept=pltpu.HBM,
        far=(0, 1, 2, 3),
        limit=67_000_000,
    )
    mine = chips_exchange(placed)
    theirs = other_core(mine)
    reorder = (
        shard_order(hidden_units)[:, None] == jnp.arange(hidden_units, dtype=jnp.int32)[None, :]
    ).astype(BF16)
    theirs, reorder = lax.optimization_barrier((theirs, reorder))

    def vmem(rows, columns=width):
        return pltpu.VMEM((rows, columns), BF16)

    matrix = 2 * ROWS * hidden_units * width
    weight_out = w_down[0]
    kept = [out((ROWS, width)), out((ROWS, 2 * hidden_units), F32)]
    own_grads, own_projected, own_hidden, weight_in = call(
        own_kernel,
        kept + [out((ROWS, hidden_units)), out((width, 2 * hidden_units))],
        mine,
        w_gate_up[0],
        scratch=[vmem(ROWS), pltpu.SemaphoreType.DMA((1,))],
        flops=2 * matrix,
        far=(1,),
        limit=50_000_000,
    )
    their_grads, their_projected, *terms = call(
        term_kernel,
        kept + [out((hidden_units // 4, width))] * 4,
        theirs,
        weight_in,
        own_hidden,
        own_grads,
        reorder,
        scratch=[vmem(ROWS), vmem(2 * ROWS, hidden_units), vmem(2 * ROWS)],
        flops=4 * matrix,
    )
    part_mine, part_theirs = call(
        partial_kernel,
        [out((ROWS, width))] * 2,
        own_grads,
        own_projected,
        their_grads,
        their_projected,
        weight_in,
        weight_out,
        scratch=[vmem(2 * ROWS, 2 * hidden_units)],
        flops=6 * matrix,
    )
    received = other_core(part_theirs)
    (joined,) = call(join_kernel, [out((N_EXPERT * CHUNK, width // 2))], part_mine, received)
    returned = chips_exchange(joined)

    both = ("z_a", "z_b")
    below = lax.ppermute(terms[3], both, BELOW)
    above = lax.ppermute(terms[2], both, ABOVE)
    passed = (terms[1].astype(F32) + below.astype(F32)).astype(BF16)
    beside = lax.ppermute(passed, "y_b", [(0, 1), (1, 0)])
    near = terms[0].astype(F32) + above.astype(F32) + beside.astype(F32)
    near = near.astype(BF16).reshape(16, hidden_units * width // (128 * N_DP), 128)
    near, returned = lax.optimization_barrier((near, returned))
    far = lax.all_to_all(near, FAR, split_axis=0, concat_axis=0, tiled=True)
    down_sum = jnp.sum(far.astype(F32) * (1.0 / N_DP), axis=0)
    (input_grad,) = call(unplace_kernel, [out((tok_count, width))], returned, ids)
    return (input_grad, down_sum[None])


def solution(mesh):
    fine = Mesh(mesh.devices.reshape(tuple(AXES.values())), ALL)
    tok = P(ALL, None)
    slab = P(("y_hi", "x", "core"), None, None)
    return jax.shard_map(
        on_device,
        mesh=fine,
        in_specs=(tok, tok, tok, tok, slab, slab),
        out_specs=(tok, P(("y_hi", "x", "core"), DP, None)),
        check_vma=False,
    )
```
